32 devices in a mesh: groups: 2 (over y), ctx: 4 (over z), head: 4 (over x, core).
Axes of the slice: x: 2, y: 2, z: 4, core: 2. Of those that a mesh axis runs over, the one named last changes fastest.
Arguments:
- tokens: bfloat16 [8192, 2048], P(('groups', 'ctx', 'head')), parts along dimension 0, may hold values from -6 to 6
- taylor_query: bfloat16 [2048, 256], P(None, 'head'), may hold values from -0.125 to 0.125
- taylor_key: bfloat16 [2048, 256], P(None, 'head'), may hold values from -0.125 to 0.125
- value_proj: bfloat16 [2048, 2048], P(None, 'head'), may hold values from -0.125 to 0.125
- window_query: bfloat16 [2048, 2048], P(None, 'head'), may hold values from -1 to 1
- window_key: bfloat16 [2048, 2048], P(None, 'head'), may hold values from -1 to 1
- out_proj: bfloat16 [2048, 2048], P('head'), may hold values from -0.125 to 0.125
- norm_gain: float32 [2048], P('head'), may hold values from 0.5 to 1.5
Outputs:
- mixer_out: bfloat16 [8192, 2048], P(('groups', 'ctx', 'head')), parts along dimension 0
The draws below stay inside these ranges and needn't reach their ends.
There are 2 independent parts, one for each index of `groups`. The reference program is written for one: setup_inputs(seed, part) draws one part's arguments, and reference() takes and returns one part's arrays. A program takes and returns all parts, laid end to end along the dimension named above; an argument that names none is the same for every part. Nothing has to cross between parts.
All inputs are finite; a program needn't handle non-finite values.
Results may differ from the reference program's by a relative error of at most 0.014.
Values may be sent and summed in bfloat16 or wider, within the bound.
A program may use at most 128 MiB of HBM per device.

```python
import math
import jax
import jax.numpy as jnp
from jax import lax

D = 2048
H = 16
FEAT = 16
DV = 128
WIN = 64
BLK = 512
SEQ = 4096
PHI = 273
N_HEAD = 4


def draw_tokens(key, part):
    base = jnp.clip(jax.random.normal(key, (SEQ, D), jnp.float32), -6.0, 6.0)
    return base.astype(jnp.bfloat16)


def window_pair(key, which):
    own = jax.random.normal(jax.random.fold_in(key, 13 + which), (D, H * DV), jnp.float32)
    mixed = own
    return jnp.clip(mixed * D ** (-0.5), -1.0, 1.0).astype(jnp.bfloat16)


def draw_window_query(key, part):
    return window_pair(key, 0)


def draw_window_key(key, part):
    return window_pair(key, 1)


def block_scale(own_key, dims, cuts, smallest, largest):
    factor_of = 1.0
    for position, parts in cuts:
        heights = jax.random.uniform(jax.random.fold_in(jax.random.fold_in(own_key, 6), position), (parts,), jnp.float32, smallest / len(cuts), largest / len(cuts))
        factor_of = factor_of * jnp.repeat(jnp.exp(heights), dims[position] // parts).reshape((-1,) + (1,) * (len(dims) - 1 - position))
    return factor_of


def scatter_about(key, shape, scale, bound, cuts=(), held_as=jnp.bfloat16):
    drawn = scale * jax.random.normal(key, shape, jnp.float32)
    if cuts:
        drawn = drawn * block_scale(key, shape, cuts, -0.22, 0.18)
    return jnp.clip(drawn, -bound, bound).astype(held_as)


def setup_inputs(seed: int = 0, part: int = 0) -> dict:
    keys = jax.random.split(jax.random.key(seed), 9)
    own_keys = jax.random.split(jax.random.fold_in(keys[8], part), 9)
    tokens = draw_tokens(jax.random.fold_in(jax.random.fold_in(keys[8], part), 71), part)
    taylor_query = scatter_about(keys[1], (D, H * FEAT), D ** -0.5, 0.125, ((1, 4),))
    taylor_key = scatter_about(keys[2], (D, H * FEAT), D ** -0.5, 0.125, ((1, 4),))
    value_proj = scatter_about(keys[3], (D, H * DV), D ** -0.5, 0.125, ((1, 4),))
    window_query = draw_window_query(jax.random.fold_in(keys[8], 71), part)
    window_key = draw_window_key(jax.random.fold_in(keys[8], 71), part)
    out_proj = scatter_about(keys[6], (H * DV, D), (H * DV) ** -0.5, 0.125, ((0, 4),))
    norm_gain = jnp.clip(0.5 + 1.0 * jax.random.uniform(keys[7], (H * DV,), jnp.float32) ** block_scale(keys[7], (H * DV,), ((0, 4),), -0.2, 0.2), 0.5, 1.5)
    return {"tokens": tokens, "taylor_query": taylor_query, "taylor_key": taylor_key, "value_proj": value_proj, "window_query": window_query, "window_key": window_key, "out_proj": out_proj, "norm_gain": norm_gain}


EPS = 1e-05

def taylor_map(vec):
    val = vec.astype(jnp.float32)
    heads = val.shape[0]
    count = val.shape[2]
    first = val * FEAT ** (-0.25)
    second = (val[:, :, None, :] * val[:, None, :, :]).reshape(heads, FEAT * FEAT, count) * (1.0 / math.sqrt(2.0 * FEAT))
    ones = jnp.ones((heads, 1, count), jnp.float32)
    return jnp.concatenate([ones, first, second], axis=1).astype(jnp.bfloat16)

def reference(tokens, taylor_query, taylor_key, value_proj, window_query, window_key, out_proj, norm_gain):

    def project(matrix):
        return jnp.dot(tokens, matrix, preferred_element_type=jnp.float32).astype(jnp.bfloat16)
    feat_q = project(taylor_query).reshape(SEQ, H, FEAT)
    feat_k = project(taylor_key).reshape(SEQ, H, FEAT)
    values = project(value_proj).reshape(SEQ, H, DV)
    win_q = project(window_query).reshape(SEQ, H, DV)
    win_k = project(window_key).reshape(SEQ, H, DV)
    zero_rows = jnp.zeros((WIN - 1, H, DV), jnp.bfloat16)
    padded_k = jnp.concatenate([zero_rows, win_k], axis=0)
    padded_v = jnp.concatenate([zero_rows, values], axis=0)
    gain = norm_gain.reshape(H, DV)
    group = H // N_HEAD
    row_pos = jnp.arange(BLK, dtype=jnp.int32)[:, None]
    col_pos = jnp.arange(BLK + WIN - 1, dtype=jnp.int32)[None, :]
    band = (col_pos <= row_pos + WIN - 1) & (col_pos >= row_pos)
    causal = jnp.arange(BLK, dtype=jnp.int32)[None, :] <= jnp.arange(BLK, dtype=jnp.int32)[:, None]

    def step(prefix, index):
        start = (index * BLK).astype(jnp.int32)

        def rows(array):
            return lax.dynamic_slice_in_dim(array, start, BLK, 0)
        block_q = rows(feat_q)
        block_k = rows(feat_k)
        block_v = rows(values)
        block_wq = rows(win_q)
        ext_k = lax.dynamic_slice_in_dim(padded_k, start, BLK + WIN - 1, 0)
        ext_v = lax.dynamic_slice_in_dim(padded_v, start, BLK + WIN - 1, 0)
        phi_q = taylor_map(jnp.transpose(block_q, (1, 2, 0)))
        phi_k = taylor_map(jnp.transpose(block_k, (1, 2, 0)))
        state_b = jnp.einsum('hpr,rhd->hpd', phi_k.astype(jnp.float32), block_v.astype(jnp.float32))
        prefix_low = lax.optimization_barrier(prefix.astype(jnp.bfloat16))
        inter = jnp.einsum('hpr,hpd->rhd', phi_q.astype(jnp.float32), prefix_low.astype(jnp.float32))
        scores = jnp.einsum('rhf,chf->hrc', block_q.astype(jnp.float32), block_k.astype(jnp.float32)) / math.sqrt(FEAT)
        weight = jnp.where(causal[None], 1.0 + scores + 0.5 * scores * scores, 0.0).astype(jnp.bfloat16)
        intra = jnp.einsum('hrc,chd->rhd', weight.astype(jnp.float32), block_v.astype(jnp.float32))
        linear = inter + intra
        normed = linear * lax.rsqrt(lax.optimization_barrier(jnp.mean(linear * linear, axis=2, keepdims=True)) + EPS) * gain[None]
        wscore = jnp.einsum('rhd,chd->hrc', block_wq.astype(jnp.float32), ext_k.astype(jnp.float32)) / math.sqrt(DV)
        key_pos = start + col_pos - (WIN - 1)
        allowed = band & (key_pos >= 0)
        wscore = jnp.where(allowed[None], wscore, -1e+30)
        top = lax.optimization_barrier(jnp.max(wscore, axis=2, keepdims=True))
        expo = jnp.exp(wscore - top)
        prob = (expo / lax.optimization_barrier(jnp.sum(expo, axis=2, keepdims=True))).astype(jnp.bfloat16)
        window = jnp.einsum('hrc,chd->rhd', prob.astype(jnp.float32), ext_v.astype(jnp.float32))
        head_out = (normed + window).astype(jnp.bfloat16).reshape(BLK, H * DV)
        total = jnp.zeros((BLK, D), jnp.float32)
        for number in range(N_HEAD):
            lower = number * group * DV
            upper = (number + 1) * group * DV
            partial_g = jnp.dot(head_out[:, lower:upper], out_proj[lower:upper], preferred_element_type=jnp.float32).astype(jnp.bfloat16)
            total = total + partial_g.astype(jnp.float32)
        return (prefix + state_b, total.astype(jnp.bfloat16))
    initial = jnp.zeros((H, PHI, DV), jnp.float32)
    final_state, outputs = lax.scan(step, initial, jnp.arange(SEQ // BLK, dtype=jnp.int32))
    return outputs.reshape(SEQ, D)
```

```python
import functools
import math

import jax
import jax.numpy as jnp
from jax import lax
from jax.experimental import pallas as pl
from jax.experimental.pallas import tpu as pltpu
from jax.sharding import PartitionSpec as P

FEAT = 16
DV = 128
WIN = 64
BLK = 512
EPS = 1e-05
MESH = pl.DeviceIdType.MESH
F32 = jnp.float32
BF16 = jnp.bfloat16
ROWS = 9 * FEAT + FEAT

NSEM = 24
S_OWN, S_ACR, S_FWD, S_SIB, S_SUM, S_HK, S_HV, S_ST, S_DIA = 0, 1, 5, 9, 10, 14, 15, 16, 20


def tn(a, b):
    return lax.dot_general(a, b, (((0,), (0,)), ((), ())), preferred_element_type=F32)


def nt(a, b):
    return lax.dot_general(a, b, (((1,), (1,)), ((), ())), preferred_element_type=F32)


def nn(a, b):
    return jnp.dot(a, b, preferred_element_type=F32)


def taylor(u, query):
    count = u.shape[1]
    pieces = []
    for d in range(9):
        other = u if d == 0 else pltpu.roll(u, FEAT - d, 0)
        piece = (u * other) * (1.0 / math.sqrt(2.0 * FEAT))
        if query and d > 0:
            piece = piece * 2.0
        pieces.append(piece)
    row = lax.broadcasted_iota(jnp.int32, (FEAT, count), 0)
    pieces[8] = jnp.where(row < FEAT // 2, pieces[8], jnp.where(row == FEAT // 2, 1.0, 0.0))
    pieces.append(u * FEAT ** (-0.25))
    return jnp.concatenate([piece.astype(BF16) for piece in pieces], axis=0)


def kernel(
    n_ctx, heads,
    tok, tq, tk, wv, wq, wk, wo, gain,
    out,
    xbuf, tq_v, tk_v, wqk_v, wv_v, wq_v, wk_v, wo_v,
    feat_t, ext_v, ext_k, win_q, lin, ho, state, inc,
    p_dia, p_acr, p_sib, p_me, r_pair, r_sib, r_acr,
    send, recv, lsem,
):
    me = lax.axis_index("head")
    ctx = lax.axis_index("ctx")
    chip, core = me // 2, lax.rem(me, 2)
    sib = chip * 2 + (1 - core)
    acr = (1 - chip) * 2 + core
    dia = (1 - chip) * 2 + (1 - core)
    rows = tok.shape[0]
    quarter = rows // 4
    half = rows // 2
    wide = heads * DV
    has_prev = ctx > 0
    has_next = ctx < n_ctx - 1

    loads = [
        pltpu.make_async_copy(src, dst, lsem.at[i])
        for i, (src, dst) in enumerate(
            ((tok, xbuf.at[me]), (tq, tq_v), (tk, tk_v), (wv, wv_v), (wq, wq_v), (wk, wk_v), (wo, wo_v))
        )
    ]
    for load in loads:
        load.start()

    barrier = pltpu.get_barrier_semaphore()
    for peer in (sib, acr):
        pl.semaphore_signal(barrier, inc=1, device_id={"head": peer}, device_id_type=MESH)

    @pl.when(has_prev)
    def _():
        pl.semaphore_signal(barrier, inc=1, device_id={"ctx": ctx - 1}, device_id_type=MESH)

    @pl.when(has_next)
    def _():
        pl.semaphore_signal(barrier, inc=1, device_id={"ctx": ctx + 1}, device_id_type=MESH)

    pl.semaphore_wait(barrier, 2 + jnp.where(has_prev, 1, 0) + jnp.where(has_next, 1, 0))

    def remote(src, dst, index, **peer):
        return pltpu.make_async_remote_copy(
            src_ref=src, dst_ref=dst, send_sem=send.at[index], recv_sem=recv.at[index],
            device_id=peer, device_id_type=MESH,
        )

    def piece(owner, i):
        return xbuf.at[owner, pl.ds(i * quarter, quarter)]

    across = [
        remote(tok.at[pl.ds(i * quarter, quarter)], piece(me, i), S_ACR + i, head=acr) for i in range(4)
    ]
    for copy in across:
        copy.start()
    to_sib = remote(tok, xbuf.at[me], S_OWN, head=sib)
    to_sib.start()
    forwards = [remote(piece(acr, i), piece(acr, i), S_FWD + i, head=sib) for i in range(4)]

    def forward(i):
        remote(piece(acr, i), piece(acr, i), S_ACR + i, head=acr).wait_recv()
        forwards[i].start()

    def project(owner, start, count, ready=lambda k: None):
        base = pl.multiple_of(owner * rows + start, count)
        spot = pl.ds(base, count)
        ext = pl.ds(pl.multiple_of(base + WIN, WIN), count)
        x = xbuf[owner, pl.ds(start, count)]
        ready(0)
        feat = nn(x, wqk_v[...]).astype(BF16).astype(F32)
        feat_t[:, spot] = feat.T.astype(BF16)
        ready(1)
        ext_v[ext, :] = nn(x, wv_v[...]).astype(BF16)
        ready(2)
        win_q[spot, :] = nn(x, wq_v[...]).astype(BF16)
        ready(3)
        ext_k[ext, :] = nn(x, wk_v[...]).astype(BF16)

    def ready(k):
        if k == 0:
            loads[1].wait()
            loads[2].wait()
            wqk_v[...] = jnp.concatenate([tq_v[...], tk_v[...]], axis=0).T
        else:
            loads[2 + k].wait()

    def head_cols(h):
        return pl.ds(pl.multiple_of(h * DV, DV), DV)

    def q_rows(h):
        return pl.ds(pl.multiple_of(h * FEAT, FEAT), FEAT)

    def k_rows(h):
        return pl.ds(pl.multiple_of((heads + h) * FEAT, FEAT), FEAT)

    def states(block):
        base = pl.multiple_of(block * BLK, BLK)

        def one(h, carry):
            phi = taylor(feat_t[k_rows(h), pl.ds(base, BLK)].astype(F32), False)
            vals = ext_v[pl.ds(pl.multiple_of(base + WIN, WIN), BLK), head_cols(h)]
            state[block, h] = nn(phi, vals)
            return carry

        lax.fori_loop(0, heads, one, 0)

    def each_head(one):
        def step(h, carry):
            one(h)
            return carry

        lax.fori_loop(0, heads, step, 0)

    def intra(block, h):
        base = pl.multiple_of(block * BLK, BLK)
        tile = BLK // 2
        results = []
        for part in range(2):
            width = (part + 1) * tile
            start = pl.multiple_of(base + part * tile, tile)
            q = feat_t[q_rows(h), pl.ds(start, tile)]
            k = feat_t[k_rows(h), pl.ds(base, width)]
            s = tn(q, k) * (1.0 / math.sqrt(FEAT))
            row = lax.broadcasted_iota(jnp.int32, (tile, width), 0) + part * tile
            col = lax.broadcasted_iota(jnp.int32, (tile, width), 1)
            weight = jnp.where(col <= row, 1.0 + s + 0.5 * s * s, 0.0).astype(BF16)
            vals = ext_v[pl.ds(pl.multiple_of(base + WIN, WIN), width), head_cols(h)]
            results.append((start, nn(weight, vals)))
        for start, result in results:
            lin[pl.ds(start, tile), head_cols(h)] = result

    def window(block, h):
        tile = 128
        span = tile + WIN
        starts = [pl.multiple_of(block * BLK + part * tile, tile) for part in range(BLK // tile)]
        row = lax.broadcasted_iota(jnp.int32, (tile, span), 0)
        col = lax.broadcasted_iota(jnp.int32, (tile, span), 1)
        ok = (col <= row + WIN) & (col > row)
        lowest = jnp.where(has_prev | (block > 0), 0, WIN)
        scores = [
            nt(win_q[pl.ds(start, tile), head_cols(h)], ext_k[pl.ds(start, span), head_cols(h)])
            for start in starts
        ]
        probs = []
        for part, s in enumerate(scores):
            seen = ok & (col >= lowest) if part == 0 else ok
            s = jnp.where(seen, s * (1.0 / math.sqrt(DV)), -1e30)
            e = jnp.exp(s - jnp.max(s, axis=1, keepdims=True))
            probs.append((e * (1.0 / jnp.sum(e, axis=1, keepdims=True))).astype(BF16))
        results = [
            nn(p, ext_v[pl.ds(start, span), head_cols(h)]) for start, p in zip(starts, probs)
        ]
        for start, result in zip(starts, results):
            ho[pl.ds(start, tile), head_cols(h)] = result

    def finish(block, h):
        base = pl.multiple_of(block * BLK, BLK)
        later = jnp.where(block > 0, 1.0, 0.0).astype(F32)
        prefix = (inc[h].astype(F32) + later * state[0, h]).astype(BF16)
        phi = taylor(feat_t[q_rows(h), pl.ds(base, BLK)].astype(F32), True)
        linear = tn(phi, prefix) + lin[pl.ds(base, BLK), head_cols(h)]
        mean = jnp.mean(linear * linear, axis=1, keepdims=True)
        normed = linear * lax.rsqrt(mean + EPS) * gain[:, head_cols(h)]
        both = normed + ho[pl.ds(base, BLK), head_cols(h)]
        ho[pl.ds(base, BLK), head_cols(h)] = both

    def out_project(owner, dst, start=0, count=rows):
        spot = pl.ds(pl.multiple_of(owner * rows + start, count), count)
        left = ho[spot, :].astype(BF16)
        columns = dst.shape[1]
        for j in range(columns // 512):
            cols = slice(j * 512, (j + 1) * 512)
            dst[start : start + count, cols] = nn(left, wo_v[:, cols]).astype(BF16)

    total = 4 * rows
    next_ctx = jnp.where(has_next, ctx + 1, ctx - 1)
    last, rim = pl.ds(total, WIN), pl.ds(0, WIN)
    halo = [
        remote(ext_k.at[last], ext_k.at[rim], S_HK, ctx=next_ctx),
        remote(ext_v.at[last], ext_v.at[rim], S_HV, ctx=next_ctx),
    ]
    chain = [remote(inc.at[heads + h], inc.at[h], S_ST + h, ctx=next_ctx) for h in range(heads)]

    def start_halo(on_chip):
        @pl.when(has_next & (chip == on_chip))
        def _():
            for copy in halo:
                copy.start()

    def await_halo(on_chip):
        @pl.when(has_prev & (chip == on_chip))
        def _():
            for copy in halo:
                copy.wait_recv()

    loads[0].wait()
    project(me, 0, rows, ready)
    remote(tok, xbuf.at[sib], S_OWN, head=sib).wait_recv()
    project(sib, 0, rows)
    start_halo(1)
    forward(0)
    states(chip)
    forward(1)
    each_head(functools.partial(intra, chip))

    def arrived(i):
        remote(piece(dia, i), piece(dia, i), S_FWD + i, head=sib).wait_recv()

    arrived(0)
    arrived(1)
    project(acr, 0, half)
    project(dia, 0, half)
    forward(2)
    forward(3)
    project(acr, half, half)
    arrived(2)
    arrived(3)
    project(dia, half, half)

    other = 1 - chip
    states(other)

    @pl.when(jnp.logical_not(has_prev))
    def _():
        ext_k[0:WIN, :] = jnp.zeros((WIN, wide), BF16)
        ext_v[0:WIN, :] = jnp.zeros((WIN, wide), BF16)
        for h in range(heads):
            inc[h] = jnp.zeros((ROWS, DV), BF16)

            @pl.when(has_next)
            def _():
                inc[heads + h] = (state[0, h] + state[1, h]).astype(BF16)
                chain[h].start()

    each_head(functools.partial(intra, other))
    await_halo(1)
    for h in range(heads):

        @pl.when(has_prev & has_next)
        def _():
            chain[h].wait_recv()
            inc[heads + h] = (inc[h].astype(F32) + state[0, h] + state[1, h]).astype(BF16)
            chain[h].start()

        window(other, h)

    start_halo(0)
    for h in range(heads):

        @pl.when(has_prev & jnp.logical_not(has_next))
        def _():
            chain[h].wait_recv()

        finish(other, h)

    loads[6].wait()
    send_dia = []
    for i in range(2):
        out_project(dia, p_dia, i * half, half)
        for k in (2 * i, 2 * i + 1):
            part = pl.ds(k * quarter, quarter)
            send_dia.append(remote(p_dia.at[part], r_pair.at[part], S_DIA + k, head=sib))
            send_dia[k].start()
        out_project(acr, p_acr, i * half, half)
    sums = []
    for i in range(4):
        send_dia[i].wait_recv()
        part = pl.ds(i * quarter, quarter)
        p_acr[part, :] = (p_acr[part, :].astype(F32) + r_pair[part, :].astype(F32)).astype(BF16)
        sums.append(remote(p_acr.at[part], r_acr.at[part], S_SUM + i, head=acr))
        sums[i].start()

    await_halo(0)
    each_head(functools.partial(window, chip))
    each_head(functools.partial(finish, chip))
    out_project(sib, p_sib)
    send_sib = remote(p_sib, r_sib, S_SIB, head=sib)
    send_sib.start()
    out_project(me, p_me)
    send_sib.wait_recv()
    for i in range(4):
        part = pl.ds(i * quarter, quarter)
        sums[i].wait_recv()
        out[part, :] = (
            p_me[part, :].astype(F32) + r_sib[part, :].astype(F32) + r_acr[part, :].astype(F32)
        ).astype(BF16)

    for copy in across + forwards + [to_sib, send_sib] + send_dia + sums:
        copy.wait_send()

    @pl.when(has_next)
    def _():
        for copy in halo + chain:
            copy.wait_send()


def per_device(n_ctx, tokens, tq, tk, wv, wq, wk, wo, gain):
    rows, depth = tokens.shape
    wide, columns = wo.shape
    heads = wide // DV
    narrow = heads * FEAT
    total = 4 * rows
    vmem = pltpu.VMEM
    return pl.pallas_call(
        functools.partial(kernel, n_ctx, heads),
        out_shape=pltpu.VMEM((rows, columns), BF16),
        in_specs=[pl.BlockSpec(memory_space=pl.ANY)] * 7 + [pl.BlockSpec(memory_space=vmem)],
        out_specs=pl.BlockSpec(memory_space=vmem),
        scratch_shapes=[
            vmem((4, rows, depth), BF16),
            vmem((narrow, depth), BF16),
            vmem((narrow, depth), BF16),
            vmem((depth, 2 * narrow), BF16),
            vmem((depth, wide), BF16),
            vmem((depth, wide), BF16),
            vmem((depth, wide), BF16),
            vmem((wide, columns), BF16),
            vmem((2 * narrow, total), BF16),
            vmem((WIN + total, wide), BF16),
            vmem((WIN + total, wide), BF16),
            vmem((total, wide), BF16),
            vmem((total, wide), F32),
            vmem((total, wide), F32),
            vmem((2, heads, ROWS, DV), F32),
            vmem((2 * heads, ROWS, DV), BF16),
        ]
        + [vmem((rows, columns), BF16)] * 7
        + [pltpu.SemaphoreType.DMA((NSEM,)), pltpu.SemaphoreType.DMA((NSEM,)), pltpu.SemaphoreType.DMA((7,))],
        compiler_params=pltpu.CompilerParams(
            collective_id=0, has_side_effects=True, vmem_limit_bytes=56 << 20
        ),
    )(tokens, tq.T, tk.T, wv, wq, wk, wo, gain.reshape(1, wide))


def solution(mesh):
    return jax.shard_map(
        functools.partial(per_device, mesh.shape["ctx"]),
        mesh=mesh,
        in_specs=(
            P(("groups", "ctx", "head"), None),
            P(None, "head"),
            P(None, "head"),
            P(None, "head"),
            P(None, "head"),
            P(None, "head"),
            P("head", None),
            P("head"),
        ),
        out_specs=P(("groups", "ctx", "head"), None),
        check_vma=False,
    )
```

```python
import functools
import math

import jax
import jax.numpy as jnp
from jax import lax
from jax.experimental import pallas as pl
from jax.experimental.pallas import tpu as pltpu
from jax.sharding import PartitionSpec as P

FEAT = 16
DV = 128
WIN = 64
BLK = 512
EPS = 1e-05
MESH = pl.DeviceIdType.MESH
F32 = jnp.float32
BF16 = jnp.bfloat16
ROWS = 9 * FEAT + FEAT

S_OWN, S_ACR, S_FWD, S_HK, S_HV, S_WSIB, S_WACR, S_WDIA, S_SIB, S_HEAD = 0, 1, 5, 9, 10, 11, 12, 13, 14, 15
RIGHT, LEFT = 0, 1


def tn(a, b):
    return lax.dot_general(a, b, (((0,), (0,)), ((), ())), preferred_element_type=F32)


def nt(a, b):
    return lax.dot_general(a, b, (((1,), (1,)), ((), ())), preferred_element_type=F32)


def nn(a, b):
    return jnp.dot(a, b, preferred_element_type=F32)


def taylor(u, query):
    count = u.shape[1]
    pieces = []
    for d in range(9):
        other = u if d == 0 else pltpu.roll(u, FEAT - d, 0)
        piece = (u * other) * (1.0 / math.sqrt(2.0 * FEAT))
        if query and d > 0:
            piece = piece * 2.0
        pieces.append(piece)
    row = lax.broadcasted_iota(jnp.int32, (FEAT, count), 0)
    pieces[8] = jnp.where(row < FEAT // 2, pieces[8], jnp.where(row == FEAT // 2, 1.0, 0.0))
    pieces.append(u * FEAT ** (-0.25))
    return jnp.concatenate([piece.astype(BF16) for piece in pieces], axis=0)


def kernel(
    n_groups, n_ctx, heads,
    tok, tq, tk, wv, wq, wk, wo, gain,
    out,
    xbuf, tq_v, tk_v, wqk_v, wv_v, wq_v, wk_v, wo_all,
    feat_t, ext_v, ext_k, win_q, lin, ho, state, inc,
    done, got, acc,
    send, recv, lsem, z_send, z_recv, y_send, y_recv,
):
    me = lax.axis_index("head")
    ctx = lax.axis_index("ctx")
    grp = lax.axis_index("groups")
    chip, core = me // 2, lax.rem(me, 2)
    sib = chip * 2 + (1 - core)
    acr = (1 - chip) * 2 + core
    dia = (1 - chip) * 2 + (1 - core)
    rows = tok.shape[0]
    quarter = rows // 4
    half = rows // 2
    wide, columns = wo.shape
    has_prev = ctx > 0
    has_next = ctx < n_ctx - 1
    next_ctx = jnp.where(has_next, ctx + 1, ctx - 1)
    prev_ctx = jnp.where(has_prev, ctx - 1, ctx + 1)

    loads = [
        pltpu.make_async_copy(src, dst, lsem.at[i])
        for i, (src, dst) in enumerate(
            ((tok, xbuf.at[me]), (tq, tq_v), (tk, tk_v), (wv, wv_v), (wq, wq_v), (wk, wk_v), (wo, wo_all.at[me]))
        )
    ]
    for load in loads:
        load.start()

    barrier = pltpu.get_barrier_semaphore()
    for peer in (acr, sib, dia):
        pl.semaphore_signal(barrier, inc=1, device_id={"head": peer}, device_id_type=MESH)
    for away in range(1, n_groups):
        pl.semaphore_signal(
            barrier, inc=1, device_id={"groups": lax.rem(grp + away, n_groups)}, device_id_type=MESH
        )

    @pl.when(has_prev)
    def _():
        pl.semaphore_signal(barrier, inc=1, device_id={"ctx": ctx - 1}, device_id_type=MESH)

    @pl.when(has_next)
    def _():
        pl.semaphore_signal(barrier, inc=1, device_id={"ctx": ctx + 1}, device_id_type=MESH)

    pl.semaphore_wait(barrier, 2 + n_groups + jnp.where(has_prev, 1, 0) + jnp.where(has_next, 1, 0))

    def remote(src, dst, index, **peer):
        return pltpu.make_async_remote_copy(
            src_ref=src, dst_ref=dst, send_sem=send.at[index], recv_sem=recv.at[index],
            device_id=peer, device_id_type=MESH,
        )

    def piece(owner, i):
        return xbuf.at[owner, pl.ds(i * quarter, quarter)]

    share_rows, share_cols = wide // n_ctx, columns // n_groups

    def share(number, group):
        return (
            pl.ds(pl.multiple_of(number * share_rows, share_rows), share_rows),
            pl.ds(pl.multiple_of(group * share_cols, share_cols), share_cols),
        )

    wo_across = remote(wo.at[share(ctx, grp)], wo_all.at[(me, *share(ctx, grp))], S_WACR, head=acr)
    wo_across.start()
    across = [
        remote(tok.at[pl.ds(i * quarter, quarter)], piece(me, i), S_ACR + i, head=acr) for i in range(4)
    ]
    for copy in across:
        copy.start()
    to_sib = remote(tok, xbuf.at[me], S_OWN, head=sib)
    to_sib.start()
    wo_sib = remote(wo, wo_all.at[me], S_WSIB, head=sib)
    wo_sib.start()
    wo_dia = remote(wo_all.at[acr], wo_all.at[acr], S_WDIA, head=sib)
    forwards = [remote(piece(acr, i), piece(acr, i), S_FWD + i, head=sib) for i in range(4)]

    def forward(i):
        remote(piece(acr, i), piece(acr, i), S_ACR + i, head=acr).wait_recv()
        forwards[i].start()

    def along(number, way):
        spot = wo_all.at[(acr, *share(number, grp))]
        return pltpu.make_async_remote_copy(
            src_ref=spot, dst_ref=spot, send_sem=z_send.at[way, number], recv_sem=z_recv.at[number],
            device_id={"ctx": next_ctx if way == RIGHT else prev_ctx}, device_id_type=MESH,
        )

    def beside(number, away, group):
        spot = wo_all.at[(acr, *share(number, group))]
        return pltpu.make_async_remote_copy(
            src_ref=spot, dst_ref=spot, send_sem=y_send.at[away - 1, number], recv_sem=y_recv.at[away - 1, number],
            device_id={"groups": lax.rem(grp + away, n_groups)}, device_id_type=MESH,
        )

    def spread_beside(number):
        for away in range(1, n_groups):
            beside(number, away, grp).start()

    def spread_own():
        wo_across.wait_recv()

        @pl.when(has_next)
        def _():
            along(ctx, RIGHT).start()

        @pl.when(has_prev)
        def _():
            along(ctx, LEFT).start()

        spread_beside(ctx)

    def spread(k):
        @pl.when(ctx >= k)
        def _():
            along(ctx - k, RIGHT).wait_recv()

            @pl.when(has_next)
            def _():
                along(ctx - k, RIGHT).start()

            spread_beside(ctx - k)

        @pl.when(ctx + k < n_ctx)
        def _():
            along(ctx + k, LEFT).wait_recv()

            @pl.when(has_prev)
            def _():
                along(ctx + k, LEFT).start()

            spread_beside(ctx + k)

    def spread_turn(turn):
        first, last = 1 + (n_ctx - 1) * turn // 3, 1 + (n_ctx - 1) * (turn + 1) // 3
        if last - first == 1:
            spread(first)
        else:
            lax.fori_loop(first, last, lambda k, carry: (spread(k), carry)[1], 0)

    def collect():
        def one(number, carry):
            for away in range(1, n_groups):
                beside(number, away, lax.rem(grp + n_groups - away, n_groups)).wait_recv()
            return carry

        lax.fori_loop(0, n_ctx, one, 0)
        wo_dia.start()

    def sent_shares():
        def one(number, carry):
            @pl.when(has_next & (number <= ctx))
            def _():
                along(number, RIGHT).wait_send()

            @pl.when(has_prev & (number >= ctx))
            def _():
                along(number, LEFT).wait_send()

            for away in range(1, n_groups):
                beside(number, away, grp).wait_send()
            return carry

        lax.fori_loop(0, n_ctx, one, 0)

    def project(owner, start, count, ready=lambda k: None):
        project_linear(owner, start, count, ready)
        project_window(owner, start, count, ready)

    def place(owner, start, count):
        base = pl.multiple_of(owner * rows + start, count)
        return pl.ds(base, count), pl.ds(pl.multiple_of(base + WIN, WIN), count)

    def project_linear(owner, start, count, ready=lambda k: None):
        spot, ext = place(owner, start, count)
        x = xbuf[owner, pl.ds(start, count)]
        ready(0)
        feat = nn(x, wqk_v[...]).astype(BF16).astype(F32)
        feat_t[:, spot] = feat.T.astype(BF16)
        ready(1)
        ext_v[ext, :] = nn(x, wv_v[...]).astype(BF16)

    def project_window(owner, start, count, ready=lambda k: None):
        spot, ext = place(owner, start, count)
        x = xbuf[owner, pl.ds(start, count)]
        ready(2)
        win_q[spot, :] = nn(x, wq_v[...]).astype(BF16)
        ready(3)
        ext_k[ext, :] = nn(x, wk_v[...]).astype(BF16)

    def ready(k):
        if k == 0:
            loads[1].wait()
            loads[2].wait()
            wqk_v[...] = jnp.concatenate([tq_v[...], tk_v[...]], axis=0).T
        else:
            loads[2 + k].wait()

    def head_cols(h):
        return pl.ds(pl.multiple_of(h * DV, DV), DV)

    def q_rows(h):
        return pl.ds(pl.multiple_of(h * FEAT, FEAT), FEAT)

    def k_rows(h):
        return pl.ds(pl.multiple_of((heads + h) * FEAT, FEAT), FEAT)

    def states(block):
        base = pl.multiple_of(block * BLK, BLK)

        def one(h, carry):
            phi = taylor(feat_t[k_rows(h), pl.ds(base, BLK)].astype(F32), False)
            vals = ext_v[pl.ds(pl.multiple_of(base + WIN, WIN), BLK), head_cols(h)]
            state[block, h] = nn(phi, vals)
            return carry

        lax.fori_loop(0, heads, one, 0)

    def states_half(block, number):
        spots = [place(2 * block + side, number * half, half) for side in range(2)]

        def one(h, carry):
            keys = jnp.concatenate([feat_t[k_rows(h), spot] for spot, _ in spots], axis=1)
            vals = jnp.concatenate([ext_v[ext, head_cols(h)] for _, ext in spots], axis=0)
            part = nn(taylor(keys.astype(F32), False), vals)
            state[block, h] = part if number == 0 else state[block, h] + part
            return carry

        lax.fori_loop(0, heads, one, 0)

    def each_head(one):
        def step(h, carry):
            one(h)
            return carry

        lax.fori_loop(0, heads, step, 0)

    def intra(block, h):
        base = pl.multiple_of(block * BLK, BLK)
        tile = BLK // 2
        results = []
        for part in range(2):
            width = (part + 1) * tile
            start = pl.multiple_of(base + part * tile, tile)
            q = feat_t[q_rows(h), pl.ds(start, tile)]
            k = feat_t[k_rows(h), pl.ds(base, width)]
            s = tn(q, k) * (1.0 / math.sqrt(FEAT))
            row = lax.broadcasted_iota(jnp.int32, (tile, width), 0) + part * tile
            col = lax.broadcasted_iota(jnp.int32, (tile, width), 1)
            weight = jnp.where(col <= row, 1.0 + s + 0.5 * s * s, 0.0).astype(BF16)
            vals = ext_v[pl.ds(pl.multiple_of(base + WIN, WIN), width), head_cols(h)]
            results.append((start, nn(weight, vals)))
        for start, result in results:
            lin[pl.ds(start, tile), head_cols(h)] = result

    def window(block, h):
        tile = 128
        span = tile + WIN
        starts = [pl.multiple_of(block * BLK + part * tile, tile) for part in range(BLK // tile)]
        row = lax.broadcasted_iota(jnp.int32, (tile, span), 0)
        col = lax.broadcasted_iota(jnp.int32, (tile, span), 1)
        ok = (col <= row + WIN) & (col > row)
        lowest = jnp.where(has_prev | (block > 0), 0, WIN)
        scores = [
            nt(win_q[pl.ds(start, tile), head_cols(h)], ext_k[pl.ds(start, span), head_cols(h)])
            for start in starts
        ]
        probs = []
        for part, s in enumerate(scores):
            seen = ok & (col >= lowest) if part == 0 else ok
            s = jnp.where(seen, s * (1.0 / math.sqrt(DV)), -1e30)
            e = jnp.exp(s - jnp.max(s, axis=1, keepdims=True))
            probs.append((e * (1.0 / jnp.sum(e, axis=1, keepdims=True))).astype(BF16))
        results = [
            nn(p, ext_v[pl.ds(start, span), head_cols(h)]) for start, p in zip(starts, probs)
        ]
        for start, result in zip(starts, results):
            ho[pl.ds(start, tile), head_cols(h)] = result

    def finish(block, h):
        base = pl.multiple_of(block * BLK, BLK)
        later = jnp.where(block > 0, 1.0, 0.0).astype(F32)
        prefix = (inc[h].astype(F32) + later * state[0, h]).astype(BF16)
        phi = taylor(feat_t[q_rows(h), pl.ds(base, BLK)].astype(F32), True)
        linear = tn(phi, prefix) + lin[pl.ds(base, BLK), head_cols(h)]
        mean = jnp.mean(linear * linear, axis=1, keepdims=True)
        normed = linear * lax.rsqrt(mean + EPS) * gain[:, head_cols(h)]
        both = normed + ho[pl.ds(base, BLK), head_cols(h)]
        done[pl.ds(base, BLK), head_cols(h)] = both.astype(BF16)

    def head_out(owner, h):
        cols = pl.ds(h * DV, DV)
        spot = pl.ds(pl.multiple_of(owner * rows, rows), rows)
        number = S_HEAD + heads * (1 if owner is acr else 2) + h
        return remote(done.at[spot, cols], got.at[me, :, cols], number, head=owner)

    def head_in(owner, h):
        cols = pl.ds(h * DV, DV)
        number = S_HEAD + heads * (1 if owner is acr else 2) + h
        return remote(got.at[owner, :, cols], got.at[owner, :, cols], number, head=owner)

    def out_project(pieces, begin, end):
        for j in range(columns // 512):
            cols = slice(j * 512, (j + 1) * 512)
            total = 0.0 if begin else acc[:, cols]
            for left, owner, first, last in pieces:
                total = total + nn(left, wo_all[owner, first:last, cols])
            if end:
                out[:, cols] = total.astype(BF16)
            else:
                acc[:, cols] = total

    total = 4 * rows
    last, rim = pl.ds(total, WIN), pl.ds(0, WIN)
    halo = [
        remote(ext_k.at[last], ext_k.at[rim], S_HK, ctx=next_ctx),
        remote(ext_v.at[last], ext_v.at[rim], S_HV, ctx=next_ctx),
    ]
    chain = [remote(inc.at[heads + h], inc.at[h], S_HEAD + h, ctx=next_ctx) for h in range(heads)]

    def start_halo(on_chip):
        @pl.when(has_next & (chip == on_chip))
        def _():
            for copy in halo:
                copy.start()

    def await_halo(on_chip):
        @pl.when(has_prev & (chip == on_chip))
        def _():
            for copy in halo:
                copy.wait_recv()

    other = 1 - chip
    loads[0].wait()
    project(me, 0, rows, ready)
    remote(tok, xbuf.at[sib], S_OWN, head=sib).wait_recv()
    project(sib, 0, rows)
    start_halo(1)
    spread_own()
    states(chip)
    each_head(functools.partial(intra, chip))
    forward(0)
    spread_turn(0)
    forward(1)

    def arrived(i):
        remote(piece(dia, i), piece(dia, i), S_FWD + i, head=sib).wait_recv()

    arrived(0)
    arrived(1)
    project(acr, 0, half)
    project(dia, 0, half)
    states_half(other, 0)
    forward(2)
    spread_turn(1)
    forward(3)
    project_linear(acr, half, half)
    arrived(2)
    arrived(3)
    project_linear(dia, half, half)
    states_half(other, 1)

    @pl.when(jnp.logical_not(has_prev))
    def _():
        ext_k[0:WIN, :] = jnp.zeros((WIN, wide), BF16)
        ext_v[0:WIN, :] = jnp.zeros((WIN, wide), BF16)
        for h in range(heads):
            inc[h] = jnp.zeros((ROWS, DV), BF16)

            @pl.when(has_next)
            def _():
                inc[heads + h] = (state[0, h] + state[1, h]).astype(BF16)
                chain[h].start()

    project_window(acr, half, half)
    project_window(dia, half, half)
    start_halo(0)
    spread_turn(2)
    each_head(functools.partial(intra, other))
    await_halo(1)
    for h in range(heads):

        @pl.when(has_prev & has_next)
        def _():
            chain[h].wait_recv()
            inc[heads + h] = (inc[h].astype(F32) + state[0, h] + state[1, h]).astype(BF16)
            chain[h].start()

        window(other, h)

    cross = []
    for h in range(heads):

        @pl.when(has_prev & jnp.logical_not(has_next))
        def _():
            chain[h].wait_recv()

        finish(other, h)
        for owner in (acr, dia):
            cross.append(head_out(owner, h))
            cross[-1].start()

    await_halo(0)
    each_head(functools.partial(window, chip))
    each_head(functools.partial(finish, chip))
    beside_rows = pl.ds(pl.multiple_of(sib * rows, rows), rows)
    own_rows = pl.ds(pl.multiple_of(me * rows, rows), rows)
    send_sib = remote(done.at[beside_rows], got.at[me], S_SIB, head=sib)
    send_sib.start()
    collect()
    loads[6].wait()
    remote(wo, wo_all.at[sib], S_WSIB, head=sib).wait_recv()
    send_sib.wait_recv()
    out_project([(done[own_rows, :], me, 0, wide), (got[sib], sib, 0, wide)], True, False)
    remote(wo_all.at[dia], wo_all.at[dia], S_WDIA, head=sib).wait_recv()
    for pair in range(heads // 2):
        for h in (2 * pair, 2 * pair + 1):
            for owner in (acr, dia):
                head_in(owner, h).wait_recv()
        first, last = 2 * pair * DV, 2 * (pair + 1) * DV
        out_project(
            [(got[owner, :, first:last], owner, first, last) for owner in (acr, dia)],
            False, pair == heads // 2 - 1,
        )

    for copy in across + forwards + [to_sib, wo_sib, wo_across, wo_dia, send_sib] + cross:
        copy.wait_send()
    sent_shares()

    @pl.when(has_next)
    def _():
        for copy in halo + chain:
            copy.wait_send()


def per_device(n_groups, n_ctx, tokens, tq, tk, wv, wq, wk, wo, gain):
    rows, depth = tokens.shape
    wide, columns = wo.shape
    heads = wide // DV
    narrow = heads * FEAT
    total = 4 * rows
    vmem, dma = pltpu.VMEM, pltpu.SemaphoreType.DMA
    return pl.pallas_call(
        functools.partial(kernel, n_groups, n_ctx, heads),
        out_shape=pltpu.VMEM((rows, columns), BF16),
        in_specs=[pl.BlockSpec(memory_space=pl.ANY)] * 7 + [pl.BlockSpec(memory_space=vmem)],
        out_specs=pl.BlockSpec(memory_space=vmem),
        scratch_shapes=[
            vmem((4, rows, depth), BF16),
            vmem((narrow, depth), BF16),
            vmem((narrow, depth), BF16),
            vmem((depth, 2 * narrow), BF16),
            vmem((depth, wide), BF16),
            vmem((depth, wide), BF16),
            vmem((depth, wide), BF16),
            vmem((4, wide, columns), BF16),
            vmem((2 * narrow, total), BF16),
            vmem((WIN + total, wide), BF16),
            vmem((WIN + total, wide), BF16),
            vmem((total, wide), BF16),
            vmem((total, wide), F32),
            vmem((total, wide), F32),
            vmem((2, heads, ROWS, DV), F32),
            vmem((2 * heads, ROWS, DV), BF16),
            vmem((total, wide), BF16),
            vmem((4, rows, wide), BF16),
            vmem((rows, columns), F32),
            dma((S_HEAD + 3 * heads,)),
            dma((S_HEAD + 3 * heads,)),
            dma((7,)),
            dma((2, n_ctx)),
            dma((n_ctx,)),
            dma((n_groups - 1, n_ctx)),
            dma((n_groups - 1, n_ctx)),
        ],
        compiler_params=pltpu.CompilerParams(
            collective_id=0, has_side_effects=True, vmem_limit_bytes=56 << 20
        ),
    )(tokens, tq.T, tk.T, wv, wq, wk, wo, gain.reshape(1, wide))


def solution(mesh):
    return jax.shard_map(
        functools.partial(per_device, mesh.shape["groups"], mesh.shape["ctx"]),
        mesh=mesh,
        in_specs=(
            P(("groups", "ctx", "head"), None),
            P(None, "head"),
            P(None, "head"),
            P(None, "head"),
            P(None, "head"),
            P(None, "head"),
            P("head", None),
            P("head"),
        ),
        out_specs=P(("groups", "ctx", "head"), None),
        check_vma=False,
    )
```

```python
import functools
import math

import jax
import jax.numpy as jnp
from jax import lax
from jax.experimental import pallas as pl
from jax.experimental.pallas import tpu as pltpu
from jax.sharding import PartitionSpec as P

FEAT = 16
DV = 128
WIN = 64
BLK = 512
EPS = 1e-05
MESH = pl.DeviceIdType.MESH
F32 = jnp.float32
BF16 = jnp.bfloat16
ROWS = 9 * FEAT + FEAT

S_OWN, S_ACR, S_FWD, S_HK, S_HV, S_WSIB, S_SIB, S_HEAD = 0, 1, 5, 9, 10, 11, 12, 13
RIGHT, LEFT = 0, 1


def tn(a, b):
    return lax.dot_general(a, b, (((0,), (0,)), ((), ())), preferred_element_type=F32)


def nt(a, b):
    return lax.dot_general(a, b, (((1,), (1,)), ((), ())), preferred_element_type=F32)


def nn(a, b):
    return jnp.dot(a, b, preferred_element_type=F32)


def taylor(u, query):
    count = u.shape[1]
    pieces = []
    for d in range(9):
        other = u if d == 0 else pltpu.roll(u, FEAT - d, 0)
        piece = (u * other) * (1.0 / math.sqrt(2.0 * FEAT))
        if query and d > 0:
            piece = piece * 2.0
        pieces.append(piece)
    row = lax.broadcasted_iota(jnp.int32, (FEAT, count), 0)
    pieces[8] = jnp.where(row < FEAT // 2, pieces[8], jnp.where(row == FEAT // 2, 1.0, 0.0))
    pieces.append(u * FEAT ** (-0.25))
    return jnp.concatenate([piece.astype(BF16) for piece in pieces], axis=0)


def kernel(
    n_groups, n_ctx, heads, shares,
    tok, tq, tk, wv, wq, wk, wo, gain,
    out,
    xbuf, tq_v, tk_v, wqk_v, wv_v, wq_v, wk_v, wo_all,
    feat_t, ext_v, ext_k, win_q, lin, ho, state, inc, before,
    done, got, acc,
    send, recv, lsem, x_send, x_recv, z_send, z_recv, y_send, y_recv, d_send, d_recv, s_send, s_recv,
):
    me = lax.axis_index("head")
    ctx = lax.axis_index("ctx")
    grp = lax.axis_index("groups")
    chip, core = me // 2, lax.rem(me, 2)
    sib = chip * 2 + (1 - core)
    acr = (1 - chip) * 2 + core
    dia = (1 - chip) * 2 + (1 - core)
    other = 1 - chip
    rows = tok.shape[0]
    quarter = rows // 4
    half = rows // 2
    wide, columns = wo.shape
    has_prev = ctx > 0
    has_next = ctx < n_ctx - 1
    next_ctx = jnp.where(has_next, ctx + 1, ctx - 1)
    prev_ctx = jnp.where(has_prev, ctx - 1, ctx + 1)
    levels = (n_ctx - 1).bit_length()

    loads = [
        pltpu.make_async_copy(src, dst, lsem.at[i])
        for i, (src, dst) in enumerate(
            ((tok, xbuf.at[me]), (tq, tq_v), (tk, tk_v), (wv, wv_v), (wq, wq_v), (wk, wk_v), (wo, wo_all.at[me]))
        )
    ]
    for load in loads:
        load.start()

    barrier = pltpu.get_barrier_semaphore()
    for peer in (acr, sib, dia):
        pl.semaphore_signal(barrier, inc=1, device_id={"head": peer}, device_id_type=MESH)
    for away in range(1, n_groups):
        pl.semaphore_signal(
            barrier, inc=1, device_id={"groups": lax.rem(grp + away, n_groups)}, device_id_type=MESH
        )

    @pl.when(has_prev)
    def _():
        pl.semaphore_signal(barrier, inc=1, device_id={"ctx": ctx - 1}, device_id_type=MESH)

    @pl.when(has_next)
    def _():
        pl.semaphore_signal(barrier, inc=1, device_id={"ctx": ctx + 1}, device_id_type=MESH)

    def giver(level):
        span = 2 << level
        return ctx // span * span + (span // 2 - 1)

    def takes(level):
        return lax.rem(ctx // (1 << level), 2) == 1

    def gives(level):
        return has_next & (lax.rem(ctx, 2 << level) == (1 << level) - 1)

    for level in range(1, levels):

        @pl.when(takes(level) & (giver(level) < ctx - 1))
        def _():
            pl.semaphore_signal(barrier, inc=1, device_id={"ctx": giver(level)}, device_id_type=MESH)

    far = sum(
        jnp.where(gives(level), jnp.minimum(1 << level, n_ctx - 1 - ctx) - 1, 0) for level in range(1, levels)
    )
    pl.semaphore_wait(barrier, 2 + n_groups + jnp.where(has_prev, 1, 0) + jnp.where(has_next, 1, 0) + far)

    def remote(src, dst, index, **peer):
        return pltpu.make_async_remote_copy(
            src_ref=src, dst_ref=dst, send_sem=send.at[index], recv_sem=recv.at[index],
            device_id=peer, device_id_type=MESH,
        )

    def piece(owner, i):
        return xbuf.at[owner, pl.ds(i * quarter, quarter)]

    share_rows, share_cols = wide // sum(shares), columns // n_groups

    def share(number, group):
        return (
            pl.ds(pl.multiple_of(number * share_rows, share_rows), share_rows),
            pl.ds(pl.multiple_of(group * share_cols, share_cols), share_cols),
        )

    def each_share(at, one):
        low = sum(jnp.where(at > i, count, 0) for i, count in enumerate(shares))
        high = sum(jnp.where(at >= i, count, 0) for i, count in enumerate(shares))

        def step(number, carry):
            one(number)
            return carry

        lax.fori_loop(low, high, step, 0)

    def wo_across(number):
        return pltpu.make_async_remote_copy(
            src_ref=wo.at[share(number, grp)], dst_ref=wo_all.at[(me, *share(number, grp))],
            send_sem=x_send.at[number], recv_sem=x_recv.at[number],
            device_id={"head": acr}, device_id_type=MESH,
        )

    each_share(ctx, lambda number: wo_across(number).start())
    across = [
        remote(tok.at[pl.ds(i * quarter, quarter)], piece(me, i), S_ACR + i, head=acr) for i in range(4)
    ]
    for copy in across:
        copy.start()
    to_sib = remote(tok, xbuf.at[me], S_OWN, head=sib)
    to_sib.start()
    wo_sib = remote(wo, wo_all.at[me], S_WSIB, head=sib)
    wo_sib.start()
    forwards = [remote(piece(acr, i), piece(acr, i), S_FWD + i, head=sib) for i in range(4)]

    def forward(i):
        remote(piece(acr, i), piece(acr, i), S_ACR + i, head=acr).wait_recv()
        forwards[i].start()

    def along(number, way):
        spot = wo_all.at[(acr, *share(number, grp))]
        return pltpu.make_async_remote_copy(
            src_ref=spot, dst_ref=spot, send_sem=z_send.at[way, number], recv_sem=z_recv.at[number],
            device_id={"ctx": next_ctx if way == RIGHT else prev_ctx}, device_id_type=MESH,
        )

    def beside(number, away, group):
        spot = wo_all.at[(acr, *share(number, group))]
        return pltpu.make_async_remote_copy(
            src_ref=spot, dst_ref=spot, send_sem=y_send.at[away - 1, number], recv_sem=y_recv.at[away - 1, number],
            device_id={"groups": lax.rem(grp + away, n_groups)}, device_id_type=MESH,
        )

    def spread_beside(number):
        for away in range(1, n_groups):
            beside(number, away, grp).start()

    def spread_own():
        def one(number):
            wo_across(number).wait_recv()

            @pl.when(has_next)
            def _():
                along(number, RIGHT).start()

            @pl.when(has_prev)
            def _():
                along(number, LEFT).start()

            spread_beside(number)

        each_share(ctx, one)

    def spread(k):
        def rightward(number):
            along(number, RIGHT).wait_recv()

            @pl.when(has_next)
            def _():
                along(number, RIGHT).start()

            spread_beside(number)

        def leftward(number):
            along(number, LEFT).wait_recv()

            @pl.when(has_prev)
            def _():
                along(number, LEFT).start()

            spread_beside(number)

        each_share(ctx - k, rightward)
        each_share(ctx + k, leftward)

    def spread_turn(turn):
        first, last = 1 + (n_ctx - 1) * turn // 3, 1 + (n_ctx - 1) * (turn + 1) // 3
        if last - first == 1:
            spread(first)
        else:
            lax.fori_loop(first, last, lambda k, carry: (spread(k), carry)[1], 0)

    def wo_pass(owner, number):
        spot = wo_all.at[owner, share(number, 0)[0]]
        return pltpu.make_async_remote_copy(
            src_ref=spot, dst_ref=spot, send_sem=d_send.at[number], recv_sem=d_recv.at[number],
            device_id={"head": sib}, device_id_type=MESH,
        )

    def collect(k):
        def one(number):
            for away in range(1, n_groups):
                beside(number, away, lax.rem(grp + n_groups - away, n_groups)).wait_recv()
            wo_pass(acr, number).start()

        each_share(ctx - k, one)
        if not (isinstance(k, int) and k == 0):
            each_share(ctx + k, one)

    def collect_turn(turn):
        first, last = 1 + (n_ctx - 1) * turn // 3, 1 + (n_ctx - 1) * (turn + 1) // 3
        if last - first == 1:
            collect(first)
        else:
            lax.fori_loop(first, last, lambda k, carry: (collect(k), carry)[1], 0)

    def each_piece(one):
        lax.fori_loop(0, sum(shares), lambda number, carry: (one(number), carry)[1], 0)

    def sent_shares():
        each_share(ctx, lambda number: wo_across(number).wait_send())
        for at in range(n_ctx):

            @pl.when(has_next & (ctx >= at))
            def _():
                each_share(at, lambda number: along(number, RIGHT).wait_send())

            @pl.when(has_prev & (ctx <= at))
            def _():
                each_share(at, lambda number: along(number, LEFT).wait_send())

        def one(number, carry):
            for away in range(1, n_groups):
                beside(number, away, grp).wait_send()
            wo_pass(acr, number).wait_send()
            return carry

        lax.fori_loop(0, sum(shares), one, 0)

    def project(owner, start, count, ready=lambda k: None):
        project_linear(owner, start, count, ready)
        project_window(owner, start, count, ready)

    def place(owner, start, count):
        base = pl.multiple_of(owner * rows + start, count)
        return pl.ds(base, count), pl.ds(pl.multiple_of(base + WIN, WIN), count)

    def project_linear(owner, start, count, ready=lambda k: None):
        spot, ext = place(owner, start, count)
        x = xbuf[owner, pl.ds(start, count)]
        ready(0)
        feat = nn(x, wqk_v[...]).astype(BF16).astype(F32)
        feat_t[:, spot] = feat.T.astype(BF16)
        ready(1)
        ext_v[ext, :] = nn(x, wv_v[...]).astype(BF16)

    def project_window(owner, start, count, ready=lambda k: None):
        spot, ext = place(owner, start, count)
        x = xbuf[owner, pl.ds(start, count)]
        ready(2)
        win_q[spot, :] = nn(x, wq_v[...]).astype(BF16)
        ready(3)
        ext_k[ext, :] = nn(x, wk_v[...]).astype(BF16)

    def both_rows(start, count):
        return jnp.concatenate([xbuf[2 * other + side, pl.ds(start, count)] for side in range(2)], axis=0)

    def put(dst, start, count, lead, result):
        result = result.astype(BF16)
        for side in range(2):
            base = pl.multiple_of((2 * other + side) * rows + lead + start, quarter)
            dst[pl.ds(base, count), :] = result[side * count : (side + 1) * count]

    def other_features(start, count):
        feat = nn(both_rows(start, count), wqk_v[...]).astype(BF16).astype(F32).T.astype(BF16)
        for side in range(2):
            spot = pl.ds(pl.multiple_of((2 * other + side) * rows + start, count), count)
            feat_t[:, spot] = feat[:, side * count : (side + 1) * count]

    def other_values(start, count):
        put(ext_v, start, count, WIN, nn(both_rows(start, count), wv_v[...]))

    def other_window(start, count):
        x = both_rows(start, count)
        put(win_q, start, count, 0, nn(x, wq_v[...]))
        put(ext_k, start, count, WIN, nn(x, wk_v[...]))

    def ready(k):
        if k == 0:
            loads[1].wait()
            loads[2].wait()
            wqk_v[...] = jnp.concatenate([tq_v[...], tk_v[...]], axis=0).T
        else:
            loads[2 + k].wait()

    def head_cols(h):
        return pl.ds(pl.multiple_of(h * DV, DV), DV)

    def q_rows(h):
        return pl.ds(pl.multiple_of(h * FEAT, FEAT), FEAT)

    def k_rows(h):
        return pl.ds(pl.multiple_of((heads + h) * FEAT, FEAT), FEAT)

    def states(block):
        base = pl.multiple_of(block * BLK, BLK)

        def one(h, carry):
            phi = taylor(feat_t[k_rows(h), pl.ds(base, BLK)].astype(F32), False)
            vals = ext_v[pl.ds(pl.multiple_of(base + WIN, WIN), BLK), head_cols(h)]
            state[block, h] = nn(phi, vals)
            return carry

        lax.fori_loop(0, heads, one, 0)

    def states_half(block, number):
        spots = [place(2 * block + side, number * half, half) for side in range(2)]

        def one(h, carry):
            keys = jnp.concatenate([feat_t[k_rows(h), spot] for spot, _ in spots], axis=1)
            vals = jnp.concatenate([ext_v[ext, head_cols(h)] for _, ext in spots], axis=0)
            part = nn(taylor(keys.astype(F32), False), vals)
            state[block, h] = part if number == 0 else state[block, h] + part
            return carry

        lax.fori_loop(0, heads, one, 0)

    def each_head(one):
        def step(h, carry):
            one(h)
            return carry

        lax.fori_loop(0, heads, step, 0)

    def intra(block, h):
        base = pl.multiple_of(block * BLK, BLK)
        tile = BLK // 2
        results = []
        for part in range(2):
            width = (part + 1) * tile
            start = pl.multiple_of(base + part * tile, tile)
            q = feat_t[q_rows(h), pl.ds(start, tile)]
            k = feat_t[k_rows(h), pl.ds(base, width)]
            s = tn(q, k) * (1.0 / math.sqrt(FEAT))
            row = lax.broadcasted_iota(jnp.int32, (tile, width), 0) + part * tile
            col = lax.broadcasted_iota(jnp.int32, (tile, width), 1)
            weight = jnp.where(col <= row, 1.0 + s + 0.5 * s * s, 0.0).astype(BF16)
            vals = ext_v[pl.ds(pl.multiple_of(base + WIN, WIN), width), head_cols(h)]
            results.append((start, nn(weight, vals)))
        for start, result in results:
            lin[pl.ds(start, tile), head_cols(h)] = result

    def window(block, h):
        tile = 128
        span = tile + WIN
        starts = [pl.multiple_of(block * BLK + part * tile, tile) for part in range(BLK // tile)]
        row = lax.broadcasted_iota(jnp.int32, (tile, span), 0)
        col = lax.broadcasted_iota(jnp.int32, (tile, span), 1)
        ok = (col <= row + WIN) & (col > row)
        lowest = jnp.where(has_prev | (block > 0), 0, WIN)
        scores = [
            nt(win_q[pl.ds(start, tile), head_cols(h)], ext_k[pl.ds(start, span), head_cols(h)])
            for start in starts
        ]
        probs = []
        for part, s in enumerate(scores):
            seen = ok & (col >= lowest) if part == 0 else ok
            s = jnp.where(seen, s * (1.0 / math.sqrt(DV)), -1e30)
            e = jnp.exp(s - jnp.max(s, axis=1, keepdims=True))
            probs.append((e * (1.0 / jnp.sum(e, axis=1, keepdims=True))).astype(BF16))
        results = [
            nn(p, ext_v[pl.ds(start, span), head_cols(h)]) for start, p in zip(starts, probs)
        ]
        for start, result in zip(starts, results):
            ho[pl.ds(start, tile), head_cols(h)] = result

    def finish(block, h):
        base = pl.multiple_of(block * BLK, BLK)
        later = jnp.where(block > 0, 1.0, 0.0).astype(F32)
        prefix = (before[h] + later * state[0, h]).astype(BF16)
        phi = taylor(feat_t[q_rows(h), pl.ds(base, BLK)].astype(F32), True)
        linear = tn(phi, prefix) + lin[pl.ds(base, BLK), head_cols(h)]
        mean = jnp.mean(linear * linear, axis=1, keepdims=True)
        normed = linear * lax.rsqrt(mean + EPS) * gain[:, head_cols(h)]
        both = normed + ho[pl.ds(base, BLK), head_cols(h)]
        done[pl.ds(base, BLK), head_cols(h)] = both.astype(BF16)

    def head_out(owner, h):
        cols = pl.ds(h * DV, DV)
        spot = pl.ds(pl.multiple_of(owner * rows, rows), rows)
        number = S_HEAD + heads * (1 if owner is acr else 2) + h
        return remote(done.at[spot, cols], got.at[me, :, cols], number, head=owner)

    def head_in(owner, h):
        cols = pl.ds(h * DV, DV)
        number = S_HEAD + heads * (1 if owner is acr else 2) + h
        return remote(got.at[owner, :, cols], got.at[owner, :, cols], number, head=owner)

    def out_project(pieces):
        for j in range(columns // 512):
            cols = slice(j * 512, (j + 1) * 512)
            acc[:, cols] = sum(nn(left, wo_all[owner, :, cols]) for left, owner in pieces)

    total = 4 * rows
    last, rim = pl.ds(total, WIN), pl.ds(0, WIN)
    halo = [
        remote(ext_k.at[last], ext_k.at[rim], S_HK, ctx=next_ctx),
        remote(ext_v.at[last], ext_v.at[rim], S_HV, ctx=next_ctx),
    ]

    def prefix_to(level, away, h):
        return pltpu.make_async_remote_copy(
            src_ref=inc.at[levels, h], dst_ref=inc.at[level, h],
            send_sem=s_send.at[away - 1, h], recv_sem=s_recv.at[level, h],
            device_id={"ctx": jnp.minimum(ctx + away, n_ctx - 1)}, device_id_type=MESH,
        )

    def each_taker(level, one):
        lax.fori_loop(
            1, jnp.minimum(1 << level, n_ctx - 1 - ctx) + 1, lambda away, carry: (one(away), carry)[1], 0
        )

    def give_prefix(level):
        @pl.when(gives(level))
        def _():
            for h in range(heads):
                total = state[0, h] + state[1, h]
                for lower in range(level):
                    prefix_to(lower, 1, h).wait_recv()
                    total = total + inc[lower, h].astype(F32)
                inc[levels, h] = total.astype(BF16)
                each_taker(level, lambda away: prefix_to(level, away, h).start())

    def take_prefix(h):
        before[h] = jnp.zeros((ROWS, DV), F32)
        for level in range(levels):
            low = 2 << level

            @pl.when(takes(level) & jnp.logical_not(has_next & (lax.rem(ctx, low) == low - 1)))
            def _():
                prefix_to(level, 1, h).wait_recv()

            @pl.when(takes(level))
            def _():
                before[h] = before[h] + inc[level, h].astype(F32)


    def start_halo(on_chip):
        @pl.when(has_next & (chip == on_chip))
        def _():
            for copy in halo:
                copy.start()

    def await_halo(on_chip):
        @pl.when(has_prev & (chip == on_chip))
        def _():
            for copy in halo:
                copy.wait_recv()

    loads[0].wait()
    project(me, 0, rows, ready)
    remote(tok, xbuf.at[sib], S_OWN, head=sib).wait_recv()
    project(sib, 0, rows)
    start_halo(1)
    spread_own()
    states(chip)
    each_head(functools.partial(intra, chip))
    forward(0)
    spread_turn(0)
    forward(1)

    def arrived(i):
        remote(piece(dia, i), piece(dia, i), S_FWD + i, head=sib).wait_recv()

    arrived(0)
    arrived(1)
    other_features(0, half)
    other_values(0, half)
    states_half(other, 0)
    other_window(0, half)
    forward(2)
    spread_turn(1)
    collect(0)
    collect_turn(0)
    arrived(2)
    other_values(half, quarter)
    other_window(half, quarter)
    forward(3)
    arrived(3)
    other_features(half, half)
    other_values(half + quarter, quarter)
    states_half(other, 1)

    @pl.when(jnp.logical_not(has_prev))
    def _():
        ext_k[0:WIN, :] = jnp.zeros((WIN, wide), BF16)
        ext_v[0:WIN, :] = jnp.zeros((WIN, wide), BF16)

    for level in range(levels):
        give_prefix(level)
    other_window(half + quarter, quarter)
    start_halo(0)
    spread_turn(2)
    await_halo(1)
    cross = []
    for h in range(heads):
        intra(other, h)
        window(other, h)

        take_prefix(h)
        finish(other, h)
        for owner in (acr, dia):
            cross.append(head_out(owner, h))
            cross[-1].start()

    await_halo(0)
    each_head(functools.partial(window, chip))
    each_head(functools.partial(finish, chip))
    beside_rows = pl.ds(pl.multiple_of(sib * rows, rows), rows)
    own_rows = pl.ds(pl.multiple_of(me * rows, rows), rows)
    send_sib = remote(done.at[beside_rows], got.at[me], S_SIB, head=sib)
    send_sib.start()
    collect_turn(1)
    collect_turn(2)
    loads[6].wait()
    remote(wo, wo_all.at[sib], S_WSIB, head=sib).wait_recv()
    send_sib.wait_recv()
    out_project([(done[own_rows, :], me), (got[sib], sib)])
    each_piece(lambda number: wo_pass(dia, number).wait_recv())
    for h in range(heads):
        cols = slice(h * DV, (h + 1) * DV)
        for owner in (acr, dia):
            head_in(owner, h).wait_recv()
        left = jnp.concatenate([got[owner, :, cols] for owner in (acr, dia)], axis=1)
        for j in range(columns // 512):
            out_cols = slice(j * 512, (j + 1) * 512)
            right = jnp.concatenate([wo_all[owner, cols, out_cols] for owner in (acr, dia)], axis=0)
            result = acc[:, out_cols] + nn(left, right)
            if h == heads - 1:
                out[:, out_cols] = result.astype(BF16)
            else:
                acc[:, out_cols] = result

    for copy in across + forwards + [to_sib, wo_sib, send_sib] + cross:
        copy.wait_send()
    sent_shares()

    @pl.when(has_next)
    def _():
        for copy in halo:
            copy.wait_send()

    for level in range(levels):

        @pl.when(gives(level))
        def _():
            for h in range(heads):
                each_taker(level, lambda away: prefix_to(level, away, h).wait_send())


def wo_shares(n_ctx):
    each = 16 // n_ctx if n_ctx <= 16 else 1
    if n_ctx % 4 or each % 4:
        return (each,) * n_ctx
    return tuple(each * count // 4 for count in (3, 4, 4, 5) for _ in range(n_ctx // 4))


def per_device(n_groups, n_ctx, tokens, tq, tk, wv, wq, wk, wo, gain):
    rows, depth = tokens.shape
    wide, columns = wo.shape
    heads = wide // DV
    narrow = heads * FEAT
    total = 4 * rows
    shares = wo_shares(n_ctx)
    levels = (n_ctx - 1).bit_length()
    vmem, dma = pltpu.VMEM, pltpu.SemaphoreType.DMA
    return pl.pallas_call(
        functools.partial(kernel, n_groups, n_ctx, heads, shares),
        out_shape=pltpu.VMEM((rows, columns), BF16),
        in_specs=[pl.BlockSpec(memory_space=pl.ANY)] * 7 + [pl.BlockSpec(memory_space=vmem)],
        out_specs=pl.BlockSpec(memory_space=vmem),
        scratch_shapes=[
            vmem((4, rows, depth), BF16),
            vmem((narrow, depth), BF16),
            vmem((narrow, depth), BF16),
            vmem((depth, 2 * narrow), BF16),
            vmem((depth, wide), BF16),
            vmem((depth, wide), BF16),
            vmem((depth, wide), BF16),
            vmem((4, wide, columns), BF16),
            vmem((2 * narrow, total), BF16),
            vmem((WIN + total, wide), BF16),
            vmem((WIN + total, wide), BF16),
            vmem((total, wide), BF16),
            vmem((total, wide), F32),
            vmem((total, wide), F32),
            vmem((2, heads, ROWS, DV), F32),
            vmem((levels + 1, heads, ROWS, DV), BF16),
            vmem((heads, ROWS, DV), F32),
            vmem((total, wide), BF16),
            vmem((4, rows, wide), BF16),
            vmem((rows, columns), F32),
            dma((S_HEAD + 3 * heads,)),
            dma((S_HEAD + 3 * heads,)),
            dma((7,)),
            dma((sum(shares),)),
            dma((sum(shares),)),
            dma((2, sum(shares))),
            dma((sum(shares),)),
            dma((n_groups - 1, sum(shares))),
            dma((n_groups - 1, sum(shares))),
            dma((sum(shares),)),
            dma((sum(shares),)),
            dma((max(1, 1 << levels >> 1), heads)),
            dma((max(1, levels), heads)),
        ],
        compiler_params=pltpu.CompilerParams(
            collective_id=0, has_side_effects=True, vmem_limit_bytes=56 << 20
        ),
    )(tokens, tq.T, tk.T, wv, wq, wk, wo, gain.reshape(1, wide))


def solution(mesh):
    return jax.shard_map(
        functools.partial(per_device, mesh.shape["groups"], mesh.shape["ctx"]),
        mesh=mesh,
        in_specs=(
            P(("groups", "ctx", "head"), None),
            P(None, "head"),
            P(None, "head"),
            P(None, "head"),
            P(None, "head"),
            P(None, "head"),
            P("head", None),
            P("head"),
        ),
        out_specs=P(("groups", "ctx", "head"), None),
        check_vma=False,
    )
```

```python
import functools
import math

import jax
import jax.numpy as jnp
from jax import lax
from jax.experimental import pallas as pl
from jax.experimental.pallas import tpu as pltpu
from jax.sharding import PartitionSpec as P

FEAT = 16
DV = 128
WIN = 64
BLK = 512
EPS = 1e-05
MESH = pl.DeviceIdType.MESH
F32 = jnp.float32
BF16 = jnp.bfloat16
ROWS = 9 * FEAT + FEAT

S_OWN, S_ACR, S_FWD, S_HK, S_HV, S_WSIB, S_SIB, S_HEAD = 0, 1, 5, 9, 10, 11, 12, 13
RIGHT, LEFT = 0, 1


def tn(a, b):
    return lax.dot_general(a, b, (((0,), (0,)), ((), ())), preferred_element_type=F32)


def nt(a, b):
    return lax.dot_general(a, b, (((1,), (1,)), ((), ())), preferred_element_type=F32)


def nn(a, b):
    return jnp.dot(a, b, preferred_element_type=F32)


def taylor(u, query):
    count = u.shape[1]
    pieces = []
    for d in range(9):
        other = u if d == 0 else pltpu.roll(u, FEAT - d, 0)
        piece = (u * other) * (1.0 / math.sqrt(2.0 * FEAT))
        if query and d > 0:
            piece = piece * 2.0
        pieces.append(piece)
    row = lax.broadcasted_iota(jnp.int32, (FEAT, count), 0)
    pieces[8] = jnp.where(row < FEAT // 2, pieces[8], jnp.where(row == FEAT // 2, 1.0, 0.0))
    pieces.append(u * FEAT ** (-0.25))
    return jnp.concatenate([piece.astype(BF16) for piece in pieces], axis=0)


def kernel(
    n_groups, n_ctx, heads, shares,
    tok, tq, tk, wv, wq, wk, wo, gain,
    out,
    xbuf, tq_v, tk_v, wqk_v, wv_v, wq_v, wk_v, wo_all,
    feat_t, feat_q, ext_v, ext_k, win_q, lin, ho, state, inc, before,
    done, got, acc,
    send, recv, lsem, x_send, x_recv, z_send, z_recv, y_send, y_recv, d_send, d_recv, s_send, s_recv,
):
    me = lax.axis_index("head")
    ctx = lax.axis_index("ctx")
    grp = lax.axis_index("groups")
    chip, core = me // 2, lax.rem(me, 2)
    sib = chip * 2 + (1 - core)
    acr = (1 - chip) * 2 + core
    dia = (1 - chip) * 2 + (1 - core)
    other = 1 - chip
    rows = tok.shape[0]
    quarter = rows // 4
    half = rows // 2
    wide, columns = wo.shape
    has_prev = ctx > 0
    has_next = ctx < n_ctx - 1
    next_ctx = jnp.where(has_next, ctx + 1, ctx - 1)
    prev_ctx = jnp.where(has_prev, ctx - 1, ctx + 1)
    levels = (n_ctx - 1).bit_length()

    loads = [
        pltpu.make_async_copy(src, dst, lsem.at[i])
        for i, (src, dst) in enumerate(
            ((tok, xbuf.at[me]), (tq, tq_v), (tk, tk_v), (wv, wv_v), (wq, wq_v), (wk, wk_v), (wo, wo_all.at[me]))
        )
    ]
    for load in loads:
        load.start()

    barrier = pltpu.get_barrier_semaphore()
    for peer in (acr, sib, dia):
        pl.semaphore_signal(barrier, inc=1, device_id={"head": peer}, device_id_type=MESH)
    for away in range(1, n_groups):
        pl.semaphore_signal(
            barrier, inc=1, device_id={"groups": lax.rem(grp + away, n_groups)}, device_id_type=MESH
        )

    @pl.when(has_prev)
    def _():
        pl.semaphore_signal(barrier, inc=1, device_id={"ctx": ctx - 1}, device_id_type=MESH)

    @pl.when(has_next)
    def _():
        pl.semaphore_signal(barrier, inc=1, device_id={"ctx": ctx + 1}, device_id_type=MESH)

    def giver(level):
        span = 2 << level
        return ctx // span * span + (span // 2 - 1)

    def takes(level):
        return lax.rem(ctx // (1 << level), 2) == 1

    def gives(level):
        return has_next & (lax.rem(ctx, 2 << level) == (1 << level) - 1)

    for level in range(1, levels):

        @pl.when(takes(level) & (giver(level) < ctx - 1))
        def _():
            pl.semaphore_signal(barrier, inc=1, device_id={"ctx": giver(level)}, device_id_type=MESH)

    far = sum(
        jnp.where(gives(level), jnp.minimum(1 << level, n_ctx - 1 - ctx) - 1, 0) for level in range(1, levels)
    )
    pl.semaphore_wait(barrier, 2 + n_groups + jnp.where(has_prev, 1, 0) + jnp.where(has_next, 1, 0) + far)

    def remote(src, dst, index, **peer):
        return pltpu.make_async_remote_copy(
            src_ref=src, dst_ref=dst, send_sem=send.at[index], recv_sem=recv.at[index],
            device_id=peer, device_id_type=MESH,
        )

    def piece(owner, i):
        return xbuf.at[owner, pl.ds(i * quarter, quarter)]

    share_rows, share_cols = wide // sum(shares), columns // n_groups

    def share(number, group):
        return (
            pl.ds(pl.multiple_of(number * share_rows, share_rows), share_rows),
            pl.ds(pl.multiple_of(group * share_cols, share_cols), share_cols),
        )

    def each_share(at, one):
        low = sum(jnp.where(at > i, count, 0) for i, count in enumerate(shares))
        high = sum(jnp.where(at >= i, count, 0) for i, count in enumerate(shares))

        def step(number, carry):
            one(number)
            return carry

        lax.fori_loop(low, high, step, 0)

    def wo_across(number):
        return pltpu.make_async_remote_copy(
            src_ref=wo.at[share(number, grp)], dst_ref=wo_all.at[(me, *share(number, grp))],
            send_sem=x_send.at[number], recv_sem=x_recv.at[number],
            device_id={"head": acr}, device_id_type=MESH,
        )

    each_share(ctx, lambda number: wo_across(number).start())
    across = [
        remote(tok.at[pl.ds(i * quarter, quarter)], piece(me, i), S_ACR + i, head=acr) for i in range(4)
    ]
    for copy in across:
        copy.start()
    to_sib = remote(tok, xbuf.at[me], S_OWN, head=sib)
    to_sib.start()
    wo_sib = remote(wo, wo_all.at[me], S_WSIB, head=sib)
    wo_sib.start()
    forwards = [remote(piece(acr, i), piece(acr, i), S_FWD + i, head=sib) for i in range(4)]

    def forward(i):
        remote(piece(acr, i), piece(acr, i), S_ACR + i, head=acr).wait_recv()
        forwards[i].start()

    def along(number, way):
        spot = wo_all.at[(acr, *share(number, grp))]
        return pltpu.make_async_remote_copy(
            src_ref=spot, dst_ref=spot, send_sem=z_send.at[way, number], recv_sem=z_recv.at[number],
            device_id={"ctx": next_ctx if way == RIGHT else prev_ctx}, device_id_type=MESH,
        )

    def beside(number, away, group):
        spot = wo_all.at[(acr, *share(number, group))]
        return pltpu.make_async_remote_copy(
            src_ref=spot, dst_ref=spot, send_sem=y_send.at[away - 1, number], recv_sem=y_recv.at[away - 1, number],
            device_id={"groups": lax.rem(grp + away, n_groups)}, device_id_type=MESH,
        )

    def spread_beside(number):
        for away in range(1, n_groups):
            beside(number, away, grp).start()

    def spread_own():
        def one(number):
            wo_across(number).wait_recv()

            @pl.when(has_next)
            def _():
                along(number, RIGHT).start()

            @pl.when(has_prev)
            def _():
                along(number, LEFT).start()

            spread_beside(number)

        each_share(ctx, one)

    def spread(k):
        def rightward(number):
            along(number, RIGHT).wait_recv()

            @pl.when(has_next)
            def _():
                along(number, RIGHT).start()

            spread_beside(number)

        def leftward(number):
            along(number, LEFT).wait_recv()

            @pl.when(has_prev)
            def _():
                along(number, LEFT).start()

            spread_beside(number)

        each_share(ctx - k, rightward)
        each_share(ctx + k, leftward)

    def spread_turn(turn):
        first, last = 1 + (n_ctx - 1) * turn // 3, 1 + (n_ctx - 1) * (turn + 1) // 3
        if last - first == 1:
            spread(first)
        else:
            lax.fori_loop(first, last, lambda k, carry: (spread(k), carry)[1], 0)

    def wo_pass(owner, number):
        spot = wo_all.at[owner, share(number, 0)[0]]
        return pltpu.make_async_remote_copy(
            src_ref=spot, dst_ref=spot, send_sem=d_send.at[number], recv_sem=d_recv.at[number],
            device_id={"head": sib}, device_id_type=MESH,
        )

    def collect(k):
        def one(number):
            for away in range(1, n_groups):
                beside(number, away, lax.rem(grp + n_groups - away, n_groups)).wait_recv()
            wo_pass(acr, number).start()

        each_share(ctx - k, one)
        if not (isinstance(k, int) and k == 0):
            each_share(ctx + k, one)

    def collect_turn(turn):
        first, last = 1 + (n_ctx - 1) * turn // 3, 1 + (n_ctx - 1) * (turn + 1) // 3
        if last - first == 1:
            collect(first)
        else:
            lax.fori_loop(first, last, lambda k, carry: (collect(k), carry)[1], 0)

    def each_piece(one):
        lax.fori_loop(0, sum(shares), lambda number, carry: (one(number), carry)[1], 0)

    def sent_shares():
        each_share(ctx, lambda number: wo_across(number).wait_send())
        for at in range(n_ctx):

            @pl.when(has_next & (ctx >= at))
            def _():
                each_share(at, lambda number: along(number, RIGHT).wait_send())

            @pl.when(has_prev & (ctx <= at))
            def _():
                each_share(at, lambda number: along(number, LEFT).wait_send())

        def one(number, carry):
            for away in range(1, n_groups):
                beside(number, away, grp).wait_send()
            wo_pass(acr, number).wait_send()
            return carry

        lax.fori_loop(0, sum(shares), one, 0)

    def project(owner, start, count, ready=lambda k: None):
        project_linear(owner, start, count, ready)
        project_window(owner, start, count, ready)

    def place(owner, start, count):
        base = pl.multiple_of(owner * rows + start, count)
        return pl.ds(base, count), pl.ds(pl.multiple_of(base + WIN, WIN), count)

    def project_linear(owner, start, count, ready=lambda k: None):
        spot, ext = place(owner, start, count)
        x = xbuf[owner, pl.ds(start, count)]
        ready(0)
        feat = nn(x, wqk_v[...]).astype(BF16).astype(F32)
        feat_t[:, spot] = feat.T.astype(BF16)
        ready(1)
        ext_v[ext, :] = nn(x, wv_v[...]).astype(BF16)

    def project_window(owner, start, count, ready=lambda k: None):
        spot, ext = place(owner, start, count)
        x = xbuf[owner, pl.ds(start, count)]
        ready(2)
        win_q[spot, :] = nn(x, wq_v[...]).astype(BF16)
        ready(3)
        ext_k[ext, :] = nn(x, wk_v[...]).astype(BF16)

    def both_rows(start, count):
        return jnp.concatenate([xbuf[2 * other + side, pl.ds(start, count)] for side in range(2)], axis=0)

    def put(dst, start, count, lead, result):
        result = result.astype(BF16)
        for side in range(2):
            base = pl.multiple_of((2 * other + side) * rows + lead + start, quarter)
            dst[pl.ds(base, count), :] = result[side * count : (side + 1) * count]

    def other_features(start, count):
        feat = nn(both_rows(start, count), wqk_v[...]).astype(BF16).astype(F32).T.astype(BF16)
        for side in range(2):
            spot = pl.ds(pl.multiple_of((2 * other + side) * rows + start, count), count)
            feat_t[:, spot] = feat[:, side * count : (side + 1) * count]

    def other_values(start, count):
        put(ext_v, start, count, WIN, nn(both_rows(start, count), wv_v[...]))

    def other_window(start, count):
        x = both_rows(start, count)
        put(win_q, start, count, 0, nn(x, wq_v[...]))
        put(ext_k, start, count, WIN, nn(x, wk_v[...]))

    def ready(k):
        if k == 0:
            loads[1].wait()
            loads[2].wait()
            wqk_v[...] = jnp.concatenate([tq_v[...], tk_v[...]], axis=0).T
        else:
            loads[2 + k].wait()

    def head_cols(h):
        return pl.ds(pl.multiple_of(h * DV, DV), DV)

    def q_rows(h):
        return pl.ds(pl.multiple_of(h * FEAT, FEAT), FEAT)

    def k_rows(h):
        return pl.ds(pl.multiple_of((heads + h) * FEAT, FEAT), FEAT)

    def states(block):
        base = pl.multiple_of(block * BLK, BLK)

        def one(h, carry):
            phi = taylor(feat_t[k_rows(h), pl.ds(base, BLK)].astype(F32), False)
            vals = ext_v[pl.ds(pl.multiple_of(base + WIN, WIN), BLK), head_cols(h)]
            state[block, h] = nn(phi, vals)
            return carry

        lax.fori_loop(0, heads, one, 0)

    def states_half(block, number):
        spots = [place(2 * block + side, number * half, half) for side in range(2)]

        def one(h, carry):
            keys = jnp.concatenate([feat_t[k_rows(h), spot] for spot, _ in spots], axis=1)
            vals = jnp.concatenate([ext_v[ext, head_cols(h)] for _, ext in spots], axis=0)
            part = nn(taylor(keys.astype(F32), False), vals)
            state[block, h] = part if number == 0 else state[block, h] + part
            return carry

        lax.fori_loop(0, heads, one, 0)

    def quarter_features(slot, start):
        feat = nn(both_rows(start, quarter), wqk_v[...]).astype(BF16).astype(F32)
        feat_q[slot] = feat.T.astype(BF16)

    def quarter_state(slot, start, h):
        spots = [
            pl.ds(pl.multiple_of((2 * other + side) * rows + WIN + start, quarter), quarter) for side in range(2)
        ]
        vals = jnp.concatenate([ext_v[spot, head_cols(h)] for spot in spots], axis=0)
        phi = taylor(feat_q[slot, k_rows(h), :].astype(F32), False)
        state[other, h] = state[other, h] + nn(phi, vals)

    def place_features(start):
        for side in range(2):
            spot = pl.ds(pl.multiple_of((2 * other + side) * rows + start, half), half)
            cols = slice(side * quarter, (side + 1) * quarter)
            feat_t[:, spot] = jnp.concatenate([feat_q[0, :, cols], feat_q[1, :, cols]], axis=1)

    def each_head(one):
        def step(h, carry):
            one(h)
            return carry

        lax.fori_loop(0, heads, step, 0)

    def intra(block, h):
        base = pl.multiple_of(block * BLK, BLK)
        tile = BLK // 2
        results = []
        for part in range(2):
            width = (part + 1) * tile
            start = pl.multiple_of(base + part * tile, tile)
            q = feat_t[q_rows(h), pl.ds(start, tile)]
            k = feat_t[k_rows(h), pl.ds(base, width)]
            s = tn(q, k) * (1.0 / math.sqrt(FEAT))
            row = lax.broadcasted_iota(jnp.int32, (tile, width), 0) + part * tile
            col = lax.broadcasted_iota(jnp.int32, (tile, width), 1)
            weight = jnp.where(col <= row, 1.0 + s + 0.5 * s * s, 0.0).astype(BF16)
            vals = ext_v[pl.ds(pl.multiple_of(base + WIN, WIN), width), head_cols(h)]
            results.append((start, nn(weight, vals)))
        for start, result in results:
            lin[pl.ds(start, tile), head_cols(h)] = result

    def window(block, h):
        tile = 128
        span = tile + WIN
        starts = [pl.multiple_of(block * BLK + part * tile, tile) for part in range(BLK // tile)]
        row = lax.broadcasted_iota(jnp.int32, (tile, span), 0)
        col = lax.broadcasted_iota(jnp.int32, (tile, span), 1)
        ok = (col <= row + WIN) & (col > row)
        lowest = jnp.where(has_prev | (block > 0), 0, WIN)
        scores = [
            nt(win_q[pl.ds(start, tile), head_cols(h)], ext_k[pl.ds(start, span), head_cols(h)])
            for start in starts
        ]
        probs = []
        for part, s in enumerate(scores):
            seen = ok & (col >= lowest) if part == 0 else ok
            s = jnp.where(seen, s * (1.0 / math.sqrt(DV)), -1e30)
            e = jnp.exp(s - jnp.max(s, axis=1, keepdims=True))
            probs.append((e * (1.0 / jnp.sum(e, axis=1, keepdims=True))).astype(BF16))
        results = [
            nn(p, ext_v[pl.ds(start, span), head_cols(h)]) for start, p in zip(starts, probs)
        ]
        for start, result in zip(starts, results):
            ho[pl.ds(start, tile), head_cols(h)] = result

    def finish(block, h):
        base = pl.multiple_of(block * BLK, BLK)
        later = jnp.where(block > 0, 1.0, 0.0).astype(F32)
        prefix = (before[h] + later * state[0, h]).astype(BF16)
        phi = taylor(feat_t[q_rows(h), pl.ds(base, BLK)].astype(F32), True)
        linear = tn(phi, prefix) + lin[pl.ds(base, BLK), head_cols(h)]
        mean = jnp.mean(linear * linear, axis=1, keepdims=True)
        normed = linear * lax.rsqrt(mean + EPS) * gain[:, head_cols(h)]
        both = normed + ho[pl.ds(base, BLK), head_cols(h)]
        done[pl.ds(base, BLK), head_cols(h)] = both.astype(BF16)

    def head_out(owner, h):
        cols = pl.ds(h * DV, DV)
        spot = pl.ds(pl.multiple_of(owner * rows, rows), rows)
        number = S_HEAD + heads * (1 if owner is acr else 2) + h
        return remote(done.at[spot, cols], got.at[me, :, cols], number, head=owner)

    def head_in(owner, h):
        cols = pl.ds(h * DV, DV)
        number = S_HEAD + heads * (1 if owner is acr else 2) + h
        return remote(got.at[owner, :, cols], got.at[owner, :, cols], number, head=owner)

    def out_project(pieces):
        for j in range(columns // 512):
            cols = slice(j * 512, (j + 1) * 512)
            acc[:, cols] = sum(nn(left, wo_all[owner, :, cols]) for left, owner in pieces)

    total = 4 * rows
    last, rim = pl.ds(total, WIN), pl.ds(0, WIN)
    halo = [
        remote(ext_k.at[last], ext_k.at[rim], S_HK, ctx=next_ctx),
        remote(ext_v.at[last], ext_v.at[rim], S_HV, ctx=next_ctx),
    ]

    def prefix_to(level, away, h):
        return pltpu.make_async_remote_copy(
            src_ref=inc.at[levels, h], dst_ref=inc.at[level, h],
            send_sem=s_send.at[away - 1, h], recv_sem=s_recv.at[level, h],
            device_id={"ctx": jnp.minimum(ctx + away, n_ctx - 1)}, device_id_type=MESH,
        )

    def each_taker(level, one):
        lax.fori_loop(
            1, jnp.minimum(1 << level, n_ctx - 1 - ctx) + 1, lambda away, carry: (one(away), carry)[1], 0
        )

    def give_prefix(level, h):
        @pl.when(gives(level))
        def _():
            total = state[0, h] + state[1, h]
            for lower in range(level):
                prefix_to(lower, 1, h).wait_recv()
                total = total + inc[lower, h].astype(F32)
            inc[levels, h] = total.astype(BF16)
            each_taker(level, lambda away: prefix_to(level, away, h).start())

    def take_prefix(h):
        before[h] = jnp.zeros((ROWS, DV), F32)
        for level in range(levels):
            low = 2 << level

            @pl.when(takes(level) & jnp.logical_not(has_next & (lax.rem(ctx, low) == low - 1)))
            def _():
                prefix_to(level, 1, h).wait_recv()

            @pl.when(takes(level))
            def _():
                before[h] = before[h] + inc[level, h].astype(F32)


    def start_halo(on_chip):
        @pl.when(has_next & (chip == on_chip))
        def _():
            for copy in halo:
                copy.start()

    def await_halo(on_chip):
        @pl.when(has_prev & (chip == on_chip))
        def _():
            for copy in halo:
                copy.wait_recv()

    loads[0].wait()
    project(me, 0, rows, ready)
    remote(tok, xbuf.at[sib], S_OWN, head=sib).wait_recv()
    project(sib, 0, rows)
    start_halo(1)
    spread_own()
    states(chip)
    each_head(functools.partial(intra, chip))
    forward(0)
    spread_turn(0)
    forward(1)

    def arrived(i):
        remote(piece(dia, i), piece(dia, i), S_FWD + i, head=sib).wait_recv()

    arrived(0)
    arrived(1)
    other_features(0, half)
    other_values(0, half)
    states_half(other, 0)
    other_window(0, half)
    forward(2)
    spread_turn(1)
    collect(0)
    collect_turn(0)
    arrived(2)
    quarter_features(0, half)
    other_values(half, quarter)
    each_head(functools.partial(quarter_state, 0, half))
    other_window(half, quarter)
    forward(3)
    arrived(3)
    quarter_features(1, half + quarter)
    other_values(half + quarter, quarter)
    for h in range(heads):
        quarter_state(1, half + quarter, h)
        give_prefix(0, h)
    for level in range(1, levels):
        for h in range(heads):
            give_prefix(level, h)
    place_features(half)

    @pl.when(jnp.logical_not(has_prev))
    def _():
        ext_k[0:WIN, :] = jnp.zeros((WIN, wide), BF16)
        ext_v[0:WIN, :] = jnp.zeros((WIN, wide), BF16)

    other_window(half + quarter, quarter)
    start_halo(0)
    spread_turn(2)
    await_halo(1)
    cross = []
    for h in range(heads):
        intra(other, h)
        window(other, h)

        take_prefix(h)
        finish(other, h)
        for owner in (acr, dia):
            cross.append(head_out(owner, h))
            cross[-1].start()

    await_halo(0)
    each_head(functools.partial(window, chip))
    each_head(functools.partial(finish, chip))
    beside_rows = pl.ds(pl.multiple_of(sib * rows, rows), rows)
    own_rows = pl.ds(pl.multiple_of(me * rows, rows), rows)
    send_sib = remote(done.at[beside_rows], got.at[me], S_SIB, head=sib)
    send_sib.start()
    collect_turn(1)
    collect_turn(2)
    loads[6].wait()
    remote(wo, wo_all.at[sib], S_WSIB, head=sib).wait_recv()
    send_sib.wait_recv()
    out_project([(done[own_rows, :], me), (got[sib], sib)])
    each_piece(lambda number: wo_pass(dia, number).wait_recv())
    for copy in across + forwards + [to_sib, wo_sib]:
        copy.wait_send()
    sent_shares()

    @pl.when(has_next)
    def _():
        for copy in halo:
            copy.wait_send()

    for level in range(levels):

        @pl.when(gives(level))
        def _():
            for h in range(heads):
                each_taker(level, lambda away: prefix_to(level, away, h).wait_send())

    for h in range(heads):
        cols = slice(h * DV, (h + 1) * DV)
        for owner in (acr, dia):
            head_in(owner, h).wait_recv()
        left = jnp.concatenate([got[owner, :, cols] for owner in (acr, dia)], axis=1)
        for j in range(columns // 512):
            out_cols = slice(j * 512, (j + 1) * 512)
            right = jnp.concatenate([wo_all[owner, cols, out_cols] for owner in (acr, dia)], axis=0)
            result = acc[:, out_cols] + nn(left, right)
            if h == heads - 1:
                out[:, out_cols] = result.astype(BF16)
            else:
                acc[:, out_cols] = result

    for copy in [send_sib] + cross:
        copy.wait_send()


def wo_shares(n_ctx):
    each = 16 // n_ctx if n_ctx <= 16 else 1
    if n_ctx % 4 or each % 4:
        return (each,) * n_ctx
    return tuple(each * count // 4 for count in (3, 4, 4, 5) for _ in range(n_ctx // 4))


def per_device(n_groups, n_ctx, tokens, tq, tk, wv, wq, wk, wo, gain):
    rows, depth = tokens.shape
    wide, columns = wo.shape
    heads = wide // DV
    narrow = heads * FEAT
    total = 4 * rows
    shares = wo_shares(n_ctx)
    levels = (n_ctx - 1).bit_length()
    vmem, dma = pltpu.VMEM, pltpu.SemaphoreType.DMA
    return pl.pallas_call(
        functools.partial(kernel, n_groups, n_ctx, heads, shares),
        out_shape=pltpu.VMEM((rows, columns), BF16),
        in_specs=[pl.BlockSpec(memory_space=pl.ANY)] * 7 + [pl.BlockSpec(memory_space=vmem)],
        out_specs=pl.BlockSpec(memory_space=vmem),
        scratch_shapes=[
            vmem((4, rows, depth), BF16),
            vmem((narrow, depth), BF16),
            vmem((narrow, depth), BF16),
            vmem((depth, 2 * narrow), BF16),
            vmem((depth, wide), BF16),
            vmem((depth, wide), BF16),
            vmem((depth, wide), BF16),
            vmem((4, wide, columns), BF16),
            vmem((2 * narrow, total), BF16),
            vmem((2, 2 * narrow, rows // 2), BF16),
            vmem((WIN + total, wide), BF16),
            vmem((WIN + total, wide), BF16),
            vmem((total, wide), BF16),
            vmem((total, wide), F32),
            vmem((total, wide), F32),
            vmem((2, heads, ROWS, DV), F32),
            vmem((levels + 1, heads, ROWS, DV), BF16),
            vmem((heads, ROWS, DV), F32),
            vmem((total, wide), BF16),
            vmem((4, rows, wide), BF16),
            vmem((rows, columns), F32),
            dma((S_HEAD + 3 * heads,)),
            dma((S_HEAD + 3 * heads,)),
            dma((7,)),
            dma((sum(shares),)),
            dma((sum(shares),)),
            dma((2, sum(shares))),
            dma((sum(shares),)),
            dma((n_groups - 1, sum(shares))),
            dma((n_groups - 1, sum(shares))),
            dma((sum(shares),)),
            dma((sum(shares),)),
            dma((max(1, 1 << levels >> 1), heads)),
            dma((max(1, levels), heads)),
        ],
        compiler_params=pltpu.CompilerParams(
            collective_id=0, has_side_effects=True, vmem_limit_bytes=56 << 20
        ),
    )(tokens, tq.T, tk.T, wv, wq, wk, wo, gain.reshape(1, wide))


def solution(mesh):
    return jax.shard_map(
        functools.partial(per_device, mesh.shape["groups"], mesh.shape["ctx"]),
        mesh=mesh,
        in_specs=(
            P(("groups", "ctx", "head"), None),
            P(None, "head"),
            P(None, "head"),
            P(None, "head"),
            P(None, "head"),
            P(None, "head"),
            P("head", None),
            P("head"),
        ),
        out_specs=P(("groups", "ctx", "head"), None),
        check_vma=False,
    )
```
